32 devices in a mesh: grp: 2 (over y), exp: 8 (over z, core), lat: 2 (over x).
Axes of the slice: x: 2, y: 2, z: 4, core: 2. Of those that a mesh axis runs over, the one named last changes fastest.
Arguments:
- tokens: bfloat16 [128, 2880], P(('grp', 'exp'), 'lat'), parts along dimension 0, may hold values from -6 to 6
- routes: int32 [128, 4], P(('grp', 'exp')), parts along dimension 0, may hold values from 0 to 7, all different within a row; in each aligned block of 8 rows (0 to 7, 8 to 15, ...) at most 5 rows name the same one
- gates: float32 [128, 4], P(('grp', 'exp')), parts along dimension 0, may hold values from 0.1 to 1
- w_gate: bfloat16 [8, 2880, 1440], P('exp', None, 'lat'), may hold values from -0.109375 to 0.109375
- w_up: bfloat16 [8, 2880, 1440], P('exp', None, 'lat'), may hold values from -0.109375 to 0.109375
- w_down: bfloat16 [8, 1440, 2880], P('exp', 'lat'), may hold values from -0.15625 to 0.15625
- w_enc: bfloat16 [2880, 32768], P('lat', 'exp'), may hold values from -0.109375 to 0.109375
- b_enc: float32 [32768], P('exp'), may hold values from -3 to 3
- w_dec: bfloat16 [32768, 2880], P('exp', 'lat'), may hold values from -0.03125 to 0.03125
- b_dec: float32 [2880], P('lat'), may hold values from -3 to 3
Outputs:
- moe_out: bfloat16 [128, 2880], P(('grp', 'exp'), 'lat'), parts along dimension 0
- codes: bfloat16 [128, 32768], P(('grp', 'lat'), 'exp'), parts along dimension 0
- error: float32 [128, 2880], P(('grp', 'exp'), 'lat'), parts along dimension 0
The draws below stay inside these ranges and needn't reach their ends.
There are 2 independent parts, one for each index of `grp`. The reference program is written for one: setup_inputs(seed, part) draws one part's arguments, and reference() takes and returns one part's arrays. A program takes and returns all parts, laid end to end along the dimension named above; an argument that names none is the same for every part. Nothing has to cross between parts.
Inputs may be any that keep to these rules, and one draw needn't show every extreme that they name: `routes`: each row names 4 different experts and every expert is named by some row. Within each aligned block of 8 rows no expert is named by more than 5 rows; in some block some expert is named by exactly 5 rows.
All inputs are finite; a program needn't handle non-finite values.
Results may differ from the reference program's by a relative error of at most 0.013.
Values may be sent and summed in bfloat16 or wider, within the bound.
No kernel may reach another device: no remote copies, remote signals or barrier semaphores. Data moves between devices by JAX's collectives and lax.ppermute only.
A program may use at most 128 MiB of HBM per device.

```python
import math
import jax
import jax.numpy as jnp
import numpy as np
from jax import lax

D = 2880
TOP = 4
EFF = 1440
L = 32768
ROW_DEV = 8
EXPERTS = 8
ROWS = 64
CAP = 5
N_EXP = 8


def levels(key, shape, cuts, smallest, top_value):
    def one(position, blocks):
        draws = jax.random.uniform(jax.random.fold_in(jax.random.fold_in(key, 6), position), (blocks,), jnp.float32, smallest / len(cuts), top_value / len(cuts))
        return jnp.repeat(jnp.exp(draws), shape[position] // blocks).reshape((-1,) + (1,) * (len(shape) - position - 1))

    factor_of = one(*cuts[0])
    for cut in cuts[1:]:
        factor_of = factor_of * one(*cut)
    return factor_of


def assign_block(rng, own, number, rows, amount, top, bound, lean):
    sequence = jax.random.permutation(rng, amount)
    crowded, ordinary = shares(amount, rows * top, bound, lean, True), shares(amount, rows * top, bound, lean, False)
    places = jnp.arange(amount)

    def named(sizes, offset_by):
        used = int((sizes > 0).sum())
        fixed = max(1, used // 4)
        moved = fixed + (places - fixed + offset_by * (used - fixed)) % max(1, amount - fixed)
        return jnp.zeros((amount,), jnp.int32).at[sequence[jnp.where(places < fixed, places, moved)]].set(jnp.asarray(sizes, jnp.int32))

    sizes = jnp.where(number % 4 == 0, named(crowded, number // 4), named(ordinary, number - number // 4 - 1))
    mixed = jax.random.permutation(jax.random.fold_in(own, 3), amount)
    giver, receiver = mixed[0:amount // 2 * 2:2], mixed[1:amount // 2 * 2:2]
    room = jnp.minimum(sizes[giver] - 1, bound - sizes[receiver]) // 2
    room = jnp.where((giver == sequence[0]) | (receiver == sequence[0]) | (sizes[receiver] == 0), 0, jnp.maximum(room, 0))
    moved = jax.random.randint(jax.random.fold_in(own, 4), (amount // 2,), 0, 1 << 20) % (room + 1)
    sizes = sizes.at[giver].add(-moved).at[receiver].add(moved)
    labels = jnp.searchsorted(jnp.cumsum(sizes), jnp.arange(rows * top), side="right").astype(jnp.int32)
    listing = labels.reshape(top, rows).T
    listing = listing[jax.random.permutation(jax.random.fold_in(own, 1), rows)]
    offset_by = jax.random.randint(jax.random.fold_in(own, 2), (rows, 1), 0, top)
    return jnp.take_along_axis(listing, (jnp.arange(top)[None, :] + offset_by) % top, axis=1)


def shares(count, total, bound, lean, full):
    loads = [(1 << 20) // math.isqrt(rank ** lean) + 1 for rank in range(1, count + 1)]
    largest = bound if full else min(bound, max(-(-total // count), total * loads[0] // sum(loads)))
    least = 1 if total - largest >= count - 1 else 0
    counts, surplus = [largest] + [least] * (count - 1), total - largest - least * (count - 1)
    while surplus > 0:
        candidates = [i for i in range(1, count) if counts[i] < largest] or [i for i in range(1, count) if counts[i] < bound]
        mass, left = sum([loads[i] for i in candidates]), surplus
        for i in candidates:
            addition = min(bound - counts[i], max(1, left * loads[i] // mass), surplus)
            counts[i] = counts[i] + addition
            surplus = surplus - addition
    return np.array(counts)


def bell_draw(key, shape, deviation, limit, shards=(), held_as=jnp.bfloat16):
    loudness = levels(key, shape, shards, -0.22, 0.18) if shards else 1.0
    array = jax.random.normal(key, shape, jnp.float32) * deviation * loudness
    return jnp.minimum(jnp.maximum(array, -limit), limit).astype(held_as)


def setup_inputs(seed: int = 0, part: int = 0) -> dict:
    splits = jax.random.split(jax.random.key(seed), 11)
    part_keys = jax.random.split(jax.random.fold_in(splits[10], part), 11)
    tokens = bell_draw(part_keys[0], (ROWS, D), 1.0, 6.0, ((0, 8), (1, 2)))
    routes_keys = jax.random.split(jax.random.fold_in(part_keys[1], 1), ROWS // ROW_DEV)
    routes_turns = jax.random.permutation(jax.random.fold_in(part_keys[1], 3), ROWS // ROW_DEV)
    routes = jax.vmap(lambda own, number: assign_block(jax.random.fold_in(part_keys[1], 2), own, number, ROW_DEV, EXPERTS, TOP, CAP, 1))(routes_keys, routes_turns).reshape((ROWS, TOP))
    gates = jnp.clip(0.1 + 0.9 * jax.random.uniform(part_keys[2], (ROWS, TOP), jnp.float32) ** levels(part_keys[2], (ROWS, TOP), ((0, 8),), -0.2, 0.2), 0.1, 1.0)
    w_gate = bell_draw(splits[3], (EXPERTS, D, EFF), D ** -0.5, 0.109375, ((0, 8), (2, 2)))
    w_up = bell_draw(splits[4], (EXPERTS, D, EFF), D ** -0.5, 0.109375, ((0, 8), (2, 2)))
    w_down = bell_draw(splits[5], (EXPERTS, EFF, D), EFF ** -0.5, 0.15625, ((0, 8), (1, 2)))
    w_enc = bell_draw(splits[6], (D, L), D ** -0.5, 0.109375, ((0, 2), (1, 8)))
    b_enc = bell_draw(splits[7], (L,), 0.5, 3.0, ((0, 8),), jnp.float32)
    w_dec = bell_draw(splits[8], (L, D), L ** -0.5, 0.03125, ((0, 8), (1, 2)))
    b_dec = bell_draw(splits[9], (D,), 0.5, 3.0, ((0, 2),), jnp.float32)
    return {"tokens": tokens, "routes": routes, "gates": gates, "w_gate": w_gate, "w_up": w_up, "w_down": w_down, "w_enc": w_enc, "b_enc": b_enc, "w_dec": w_dec, "b_dec": b_dec}


def swiglu_expert(packed):
    buffer, gate_w, up_w, down_w = packed
    gate_sum = jnp.dot(buffer, gate_w, preferred_element_type=jnp.float32)
    up_sum = jnp.dot(buffer, up_w, preferred_element_type=jnp.float32)
    hidden = (gate_sum * jax.nn.sigmoid(1.702 * gate_sum) * (up_sum + 1.0)).astype(jnp.bfloat16)
    return jnp.dot(hidden, down_w, preferred_element_type=jnp.float32)


def reference(tokens, routes, gates, w_gate, w_up, w_down, w_enc, b_enc, w_dec, b_dec):
    flat_expert = routes.reshape(N_EXP, ROW_DEV * TOP).astype(jnp.int32)
    onehot = (flat_expert[:, :, None] == jnp.arange(EXPERTS, dtype=jnp.int32)[None, None, :]).astype(jnp.int32)
    before = jnp.cumsum(onehot, axis=1) - onehot
    rank_in = jnp.sum(before * onehot, axis=2).astype(jnp.int32)
    source = jnp.arange(N_EXP, dtype=jnp.int32)[:, None]
    slot_index = (flat_expert * (N_EXP * CAP) + source * CAP + rank_in).reshape(-1).astype(jnp.int32)
    repeated = jnp.repeat(tokens, TOP, axis=0)
    buffer = jnp.zeros((EXPERTS * N_EXP * CAP, D), jnp.bfloat16).at[slot_index].set(repeated)
    buffer = buffer.reshape(EXPERTS, N_EXP * CAP, D)
    outputs = lax.map(swiglu_expert, (buffer, w_gate, w_up, w_down))
    picked = jnp.take(outputs.reshape(EXPERTS * N_EXP * CAP, D), slot_index, axis=0).reshape(ROWS, TOP, D)
    moe_out = jnp.sum(picked * gates[:, :, None], axis=1).astype(jnp.bfloat16)
    pre = jnp.dot(tokens, w_enc, preferred_element_type=jnp.float32) + b_enc[None, :]
    codes = jnp.maximum(pre, 0.0).astype(jnp.bfloat16)
    recon = jnp.dot(codes, w_dec, preferred_element_type=jnp.float32) + b_dec[None, :]
    error = moe_out.astype(jnp.float32) - recon
    return (moe_out, codes, error)
```

```python
import jax
import jax.numpy as jnp
from jax import lax
from jax.experimental import pallas as pl
from jax.experimental.pallas import tpu as pltpu
from jax.sharding import PartitionSpec as P


VMEM = pl.BlockSpec(memory_space=pltpu.VMEM)
ANY = pl.BlockSpec(memory_space=pl.ANY)
F32 = jnp.float32
BF16 = jnp.bfloat16
CHUNKS = 4
LANES = 128
NT = (((1,), (1,)), ((), ()))


def call(body, name, out, *args, specs=None, vmem=4 << 20, flops=0, moved=0, scratch=()):
    many = isinstance(out, (list, tuple))
    return pl.pallas_call(
        body,
        name=name,
        out_shape=out,
        in_specs=list(specs) if specs else [VMEM] * len(args),
        out_specs=[VMEM] * len(out) if many else VMEM,
        scratch_shapes=list(scratch),
        compiler_params=pltpu.CompilerParams(vmem_limit_bytes=vmem),
        cost_estimate=pl.CostEstimate(flops=flops, bytes_accessed=moved, transcendentals=0),
    )(*args)


def shape(dims, dtype):
    return jax.ShapeDtypeStruct(tuple(dims), dtype)


def exact_parts(values):
    high = lax.reduce_precision(values, 8, 7)
    rest = values - high
    middle = lax.reduce_precision(rest, 8, 7)
    low = rest - middle
    return jnp.concatenate([high, middle, low], axis=1).astype(BF16)


def first_kernel(x_ref, o_ref):
    o_ref[...] = jnp.zeros_like(o_ref)


def encode_kernel(c, width, own_ref, other_ref, w_ref, kept_ref, sent_ref):
    rows = jnp.concatenate([own_ref[...], other_ref[...]], axis=0)
    part = jnp.dot(rows, w_ref[:, c * width : (c + 1) * width], preferred_element_type=F32)
    kept_ref[...] = part
    sent_ref[...] = part.astype(BF16)


def codes_of(kept, got, bias):
    return jnp.maximum(kept + got.astype(F32) + bias, 0.0).astype(BF16)


def decode_kernel(c, width, last, kept_ref, got_ref, bias_ref, w_ref, *rest):
    columns = slice(c * width, (c + 1) * width)
    codes = codes_of(kept_ref[...], got_ref[...], bias_ref[:, columns])
    total = lax.dot_general(codes, w_ref[:, columns], NT, preferred_element_type=F32)
    if c:
        total = total + rest[0][...]
        rest = rest[1:]
    if last:
        half = total.shape[0] // 2
        rest[0][...] = total[:half]
        rest[1][...] = total[half:].astype(BF16)
    else:
        rest[0][...] = total


def expert_kernel(
    experts, own_ref, other_ref, far_ref, far_other_ref, gate_ref, up_ref, down_ref,
    kept_ref, sent_ref, rows_ref,
):
    features = own_ref.shape[1]
    half = own_ref.shape[0]
    lat = lax.axis_index("lat")
    mine = lax.axis_index("exp")

    def place(near, far):
        rows_ref[:half, near : near + features] = own_ref[...]
        rows_ref[half:, near : near + features] = other_ref[...]
        rows_ref[:half, far : far + features] = far_ref[:, :features]
        rows_ref[half:, far : far + features] = far_other_ref[:, :features]

    @pl.when(lat == 0)
    def _():
        place(0, features)

    @pl.when(lat == 1)
    def _():
        place(features, 0)

    rows = rows_ref[...]
    gate_sum = lax.dot_general(rows, gate_ref[...], NT, preferred_element_type=F32)
    up_sum = lax.dot_general(rows, up_ref[...], NT, preferred_element_type=F32)
    hidden = (gate_sum * jax.nn.sigmoid(1.702 * gate_sum) * (up_sum + 1.0)).astype(BF16)
    value = jnp.dot(hidden, down_ref[...], preferred_element_type=F32)
    table = jnp.concatenate([far_ref[:, features:], far_other_ref[:, features:]], axis=0)
    table = table.astype(F32)
    lane = lax.broadcasted_iota(jnp.int32, table.shape, 1)
    chosen = (lane == mine) | (lane == mine + experts) | (lane == mine + 2 * experts)
    weight = jnp.sum(jnp.where(chosen, table, 0.0), axis=1, keepdims=True)
    value = value * weight
    kept_ref[...] = value[:half]
    sent_ref[...] = value[half:].astype(BF16)


def split_kernel(kept_ref, got_ref, mine_ref, sent_ref):
    features = mine_ref.shape[1]
    lat = lax.axis_index("lat")

    def split(near, far):
        mine_ref[...] = kept_ref[:, near : near + features] + got_ref[
            :, near : near + features
        ].astype(F32)
        sent_ref[...] = (
            kept_ref[:, far : far + features] + got_ref[:, far : far + features].astype(F32)
        ).astype(BF16)

    @pl.when(lat == 0)
    def _():
        split(0, features)

    @pl.when(lat == 1)
    def _():
        split(features, 0)


def block_kernel(count, r_ref, r_got_ref, m_ref, m_got_ref, r_own_ref, m_own_ref, *sent_refs):
    recon = r_ref[...] + r_got_ref[...].astype(F32)
    moe = m_ref[...] + m_got_ref[...].astype(F32)
    rows = recon.shape[0] // count
    r_own_ref[...] = recon[:rows]
    m_own_ref[...] = moe[:rows]
    for k in range(1, count):
        part = slice(k * rows, (k + 1) * rows)
        sent_refs[k - 1][...] = jnp.concatenate([recon[part], moe[part]], axis=0).astype(BF16)


def final_kernel(r_ref, m_ref, bias_ref, *rest):
    moe_ref, error_ref = rest[-2:]
    recon, moe = r_ref[...], m_ref[...]
    rows = recon.shape[0]
    for got in rest[:-3]:
        value = got[...].astype(F32)
        recon = recon + value[:rows]
        moe = moe + value[rows:]
    moe = moe.astype(BF16)
    moe_ref[...] = moe
    error_ref[...] = moe.astype(F32) - (recon + bias_ref[...])


def codes_kernel(zs, rows, *refs):
    bias_ref, out_ref = refs[-2:]
    pairs = refs[:-2]
    width = pairs[0].shape[1]
    lat = lax.axis_index("lat")
    mine = lax.axis_index("exp")
    blocks = out_ref.shape[0] // rows
    for c in range(len(pairs) // 2):
        kept_ref, got_ref = pairs[2 * c], pairs[2 * c + 1]
        columns = slice(c * width, (c + 1) * width)
        values = []
        for j in range(blocks):
            apart = (lat * blocks + j) ^ mine
            place = pl.multiple_of(((apart & 1) * zs + (apart >> 1)) * rows, rows)
            values.append(
                kept_ref[pl.ds(place, rows), :] + got_ref[pl.ds(place, rows), :].astype(F32)
            )
        value = jnp.concatenate(values, axis=0) + bias_ref[:, columns]
        out_ref[:, columns] = jnp.maximum(value, 0.0).astype(BF16)


def paired_device(tokens, routes, gates, w_gate, w_up, w_down, w_enc, b_enc, w_dec, b_dec):
    rows, features = tokens.shape
    experts = lax.axis_size("exp")
    zs = experts // 2
    half = rows * zs
    total_rows = 2 * half
    latents = w_enc.shape[1]
    hidden = w_gate.shape[2]
    width = latents // CHUNKS

    def over_lat(value):
        return lax.ppermute(value, "lat", [(0, 1), (1, 0)])

    def over_exp(value, apart):
        return lax.ppermute(value, "exp", [(i, i ^ apart) for i in range(experts)])

    token = call(
        first_kernel, "first", shape((8, LANES), F32), tokens, specs=[ANY],
        flops=4 * 10**9, moved=64 << 20,
    )
    tokens, token = lax.optimization_barrier((tokens, token))

    w_gate_t = jnp.swapaxes(w_gate[0], 0, 1)
    w_up_t = jnp.swapaxes(w_up[0], 0, 1)
    w_dec_t = jnp.swapaxes(w_dec, 0, 1)
    bias_enc = b_enc.reshape(1, -1)
    bias_dec = b_dec.reshape(1, -1)

    ids = jnp.arange(experts, dtype=jnp.int32)
    table = jnp.sum(
        jnp.where(routes[:, :, None] == ids[None, None, :], gates[:, :, None], 0.0), axis=1
    )
    parts = exact_parts(table)
    pad = -(features + parts.shape[1]) % LANES
    parts = jnp.pad(parts, ((0, 0), (0, pad)))

    far = over_lat(tokens)
    own = jnp.concatenate([tokens] + [over_exp(tokens, 2 * k) for k in range(1, zs)], axis=0)
    far = jnp.concatenate([far, parts], axis=1)
    far = jnp.concatenate([far] + [over_exp(far, 2 * k) for k in range(1, zs)], axis=0)
    other = over_exp(own, 1)
    far_other = over_exp(far, 1)

    kept, sent, got = [], [], []
    for c in range(CHUNKS):
        k, s = call(
            lambda *refs, c=c: encode_kernel(c, width, *refs), f"encode{c}",
            (shape((total_rows, width), F32), shape((total_rows, width), BF16)),
            own, other, w_enc,
            flops=2 * total_rows * features * width, moved=2 * features * width,
        )
        kept.append(k)
        sent.append(s)
        got.append(over_lat(s))
    far, far_other, sent[-1] = lax.optimization_barrier((far, far_other, sent[-1]))

    y_kept, y_sent = call(
        lambda *refs: expert_kernel(experts, *refs), "expert",
        (shape((half, 2 * features), F32), shape((half, 2 * features), BF16)),
        own, other, far, far_other, w_gate_t, w_up_t, w_down[0],
        scratch=[pltpu.VMEM((total_rows, 2 * features), BF16)],
        flops=12 * total_rows * features * hidden, moved=12 * features * hidden,
    )
    m_kept, m_sent = call(
        split_kernel, "split", (shape((half, features), F32), shape((half, features), BF16)),
        y_kept, over_exp(y_sent, 1), moved=12 * half * features,
    )
    m_got = over_lat(m_sent)

    got[0], y_sent = lax.optimization_barrier((got[0], y_sent))
    got[1], m_sent = lax.optimization_barrier((got[1], m_sent))
    total = None
    for c in range(CHUNKS):
        last = c == CHUNKS - 1
        args = [kept[c], got[c], bias_enc, w_dec_t] + ([total] if c else [])
        out = (
            (shape((half, features), F32), shape((half, features), BF16))
            if last
            else shape((total_rows, features), F32)
        )
        total = call(
            lambda *refs, c=c, last=last: decode_kernel(c, width, last, *refs), f"decode{c}",
            out, *args,
            flops=2 * total_rows * features * width, moved=2 * features * width,
        )
    r_kept, r_sent = total
    r_got = over_exp(r_sent, 1)

    blocks = call(
        lambda *refs: block_kernel(zs, *refs), "block",
        (shape((rows, features), F32),) * 2 + (shape((2 * rows, features), BF16),) * (zs - 1),
        r_kept, r_got, m_kept, m_got, moved=12 * half * features,
    )
    arrived = [over_exp(blocks[1 + k], 2 * k) for k in range(1, zs)]
    moe_out, error = call(
        final_kernel, "final", (shape((rows, features), BF16), shape((rows, features), F32)),
        blocks[0], blocks[1], bias_dec, *arrived, token,
        specs=[VMEM] * (3 + len(arrived)) + [ANY], moved=12 * rows * features,
    )
    pairs = [value for pair in zip(kept, got) for value in pair]
    codes = call(
        lambda *refs: codes_kernel(zs, rows, *refs), "codes", shape((half, latents), BF16),
        *pairs, bias_enc, moved=12 * half * latents,
    )
    return (moe_out, codes, error)


def expert_hidden(gate_sum, up_sum):
    return (gate_sum * jax.nn.sigmoid(1.702 * gate_sum) * (up_sum + 1.0)).astype(jnp.bfloat16)


def combine_rows(returned, slot_index, gates):
    row_count = gates.shape[0]
    top_count = gates.shape[1]
    picked = jnp.take(returned, slot_index, axis=0).reshape(row_count, top_count, returned.shape[1])
    return jnp.sum(picked * gates[:, :, None], axis=1)


def per_device(tokens, routes, gates, w_gate, w_up, w_down, w_enc, b_enc, w_dec, b_dec):
    row_count = tokens.shape[0]
    top_count = routes.shape[1]
    experts = lax.axis_size("exp")
    slots_per = min(row_count, row_count * top_count // experts + 1)
    total_slots = experts * slots_per
    flat_expert = routes.reshape(-1)
    onehot = (flat_expert[:, None] == jnp.arange(experts, dtype=jnp.int32)[None, :]).astype(
        jnp.int32
    )
    before = jnp.cumsum(onehot, axis=0) - onehot
    rank_in = jnp.sum(before * onehot, axis=1)
    slot_index = flat_expert * slots_per + rank_in
    placing = (jnp.arange(total_slots, dtype=jnp.int32)[:, None] == slot_index[None, :]).astype(
        jnp.bfloat16
    )
    outgoing = jnp.dot(
        placing, jnp.repeat(tokens, top_count, axis=0), preferred_element_type=jnp.float32
    ).astype(jnp.bfloat16)
    arrived = lax.all_to_all(outgoing, "exp", split_axis=0, concat_axis=0, tiled=True)
    block_in = lax.all_gather(arrived, "lat", axis=1, tiled=True)
    gate_rows = w_gate[0]
    up_rows = w_up[0]
    gate_sum = jnp.dot(block_in, gate_rows, preferred_element_type=jnp.float32)
    up_sum = jnp.dot(block_in, up_rows, preferred_element_type=jnp.float32)
    hidden = expert_hidden(gate_sum, up_sum)
    partial_value = jnp.dot(hidden, w_down[0], preferred_element_type=jnp.float32)
    gathered = lax.all_gather(tokens, "exp", axis=0, tiled=True)
    block_in = gathered
    pre = lax.psum_scatter(
        jnp.dot(block_in, w_enc, preferred_element_type=jnp.float32),
        "lat",
        scatter_dimension=0,
        tiled=True,
    )
    codes = jnp.maximum(pre + b_enc[None, :], 0.0).astype(jnp.bfloat16)
    shares = lax.psum_scatter(partial_value, "lat", scatter_dimension=1, tiled=True)
    returned = lax.all_to_all(shares, "exp", split_axis=0, concat_axis=0, tiled=True)
    moe_local = combine_rows(returned, slot_index, gates)
    moe_out = moe_local.astype(jnp.bfloat16)
    partial_recon = jnp.dot(
        lax.all_gather(codes, "lat", axis=0, tiled=True), w_dec, preferred_element_type=jnp.float32
    )
    recon = (
        lax.psum_scatter(
            partial_recon.astype(jnp.bfloat16), "exp", scatter_dimension=0, tiled=True
        ).astype(jnp.float32)
        + b_dec[None, :]
    )
    error = moe_out.astype(jnp.float32) - recon
    return (moe_out, codes, error)


def solution(mesh):
    placed = (
        P(("grp", "exp"), "lat"),
        P(("grp", "exp"), None),
        P(("grp", "exp"), None),
        P("exp", None, "lat"),
        P("exp", None, "lat"),
        P("exp", "lat", None),
        P("lat", "exp"),
        P("exp"),
        P("exp", "lat"),
        P("lat"),
    )
    experts = mesh.shape["exp"]
    paired = mesh.shape["lat"] == 2 and experts >= 4 and experts & (experts - 1) == 0
    return jax.shard_map(
        paired_device if paired else per_device,
        mesh=mesh,
        in_specs=placed,
        out_specs=(P(("grp", "exp"), "lat"), P(("grp", "lat"), "exp"), P(("grp", "exp"), "lat")),
        check_vma=False,
    )
```
